128 devices in a mesh: dp: 8 (over y, z_hi), mp: 16 (over z_lo, x, core).
Axes of the slice: x: 4, y: 4, z: 4 (z_hi: 2, z_lo: 2; z = z_hi * 2 + z_lo), core: 2. Of those that a mesh axis runs over, the one named last changes fastest.
Arguments:
- context: bfloat16 [512, 8192], P('dp', 'mp'), may hold values from -6 to 6
- attn_weight: bfloat16 [8192, 5120], P('mp', 'dp'), may hold values from -0.0625 to 0.0625
- stream: bfloat16 [512, 5120], P(('dp', 'mp')), may hold values from -6 to 6
- norm_gain: float32 [5120], replicated, may hold values from 0.1 to 1.9
- router_weight: bfloat16 [16, 5120], replicated, may hold values from -0.078125 to 0.078125
- expert_weights: bfloat16 [16, 3, 1536, 5120], P('mp', None, 'dp'), may hold values from -0.078125 to 0.078125
- inference_slot: int32 [16], replicated, may hold values from 0 to 15, each once
- routes: int32 [512, 6], P(('dp', 'mp')), may hold values from 0 to 15, all different within a row; in each aligned block of 4 rows (0 to 3, 4 to 7, ...) at most 2 rows name the same one
Outputs:
- hidden_out: bfloat16 [512, 5120], P(('dp', 'mp'))
- expert_mix: bfloat16 [512, 5120], P(('dp', 'mp'))
- placed_experts: bfloat16 [16, 3, 1536, 5120], P(None, None, ('dp', 'mp'))
The draws below stay inside these ranges and needn't reach their ends.
Inputs may be any that keep to these rules, and one draw needn't show every extreme that they name: inference_slot names each position once. `routes`: each row names 6 different experts. Within the rows of one device no expert is named by more than 2 rows, and in every draw some device names some expert exactly 2 times.
All inputs are finite; a program needn't handle non-finite values.
Results may differ from the reference program's by a relative error of at most 0.015.
Values may be sent and summed in bfloat16 or wider, within the bound.
No kernel may reach another device: no remote copies, remote signals or barrier semaphores. Data moves between devices by JAX's collectives and lax.ppermute only.
A program may use at most 128 MiB of HBM per device.

```python
import math
import jax
import jax.numpy as jnp
import numpy as np
from jax import lax

D = 5120
FF = 1536
TOP = 6
ROWS_DEV = 4
EXPERTS = 16
CAP = 2
HV = 8192
ROWS = 512
N_DP = 8
N_MP = 16


def levels(own_key, dims, cuts, smallest, top_value):
    gain, own = 1.0, jax.random.fold_in(own_key, 6)
    for axis_at, blocks in cuts:
        draws = jnp.exp(jax.random.uniform(jax.random.fold_in(own, axis_at), (blocks,), jnp.float32, smallest / len(cuts), top_value / len(cuts)))
        gain = gain * jnp.repeat(draws, dims[axis_at] // blocks).reshape([-1 if axis == axis_at else 1 for axis in range(len(dims))])
    return gain


def shared_out(key, own, number, rows, number_of, top, reach, lean):
    ranking = jax.random.permutation(key, number_of)
    packed, ordinary = load_shares(number_of, rows * top, reach, lean, True), load_shares(number_of, rows * top, reach, lean, False)
    places = jnp.arange(number_of)

    def named(lengths, rotation):
        used = int((lengths > 0).sum())
        fixed = max(1, used // 4)
        shifted = fixed + (places - fixed + rotation * (used - fixed)) % max(1, number_of - fixed)
        return jnp.zeros((number_of,), jnp.int32).at[ranking[jnp.where(places < fixed, places, shifted)]].set(jnp.asarray(lengths, jnp.int32))

    lengths = jnp.where(number % 4 == 0, named(packed, number // 4), named(ordinary, number - number // 4 - 1))
    mixed = jax.random.permutation(jax.random.fold_in(own, 3), number_of)
    donor, sink = mixed[0:number_of // 2 * 2:2], mixed[1:number_of // 2 * 2:2]
    margin = jnp.minimum(lengths[donor] - 1, reach - lengths[sink]) // 2
    margin = jnp.where((donor == ranking[0]) | (sink == ranking[0]) | (lengths[sink] == 0), 0, jnp.maximum(margin, 0))
    shifted = jax.random.randint(jax.random.fold_in(own, 4), (number_of // 2,), 0, 1 << 20) % (margin + 1)
    lengths = lengths.at[donor].add(-shifted).at[sink].add(shifted)
    labels = jnp.searchsorted(jnp.cumsum(lengths), jnp.arange(rows * top), side="right").astype(jnp.int32)
    listing = labels.reshape(top, rows).T
    listing = listing[jax.random.permutation(jax.random.fold_in(own, 1), rows)]
    rotation = jax.random.randint(jax.random.fold_in(own, 2), (rows, 1), 0, top)
    return jnp.take_along_axis(listing, (jnp.arange(top)[None, :] + rotation) % top, axis=1)


def load_shares(number_of, total, bound, slope, full):
    weights = [(1 << 20) // math.isqrt(standing ** slope) + 1 for standing in range(1, number_of + 1)]
    largest = bound if full else min(bound, max(-(-total // number_of), total * weights[0] // sum(weights)))
    least = 1 if total - largest >= number_of - 1 else 0
    holding, surplus = [largest] + [least] * (number_of - 1), total - largest - least * (number_of - 1)
    while surplus > 0:
        free = [i for i in range(1, number_of) if holding[i] < largest] or [i for i in range(1, number_of) if holding[i] < bound]
        pool, left = sum([weights[i] for i in free]), surplus
        for i in free:
            more = min(bound - holding[i], max(1, left * weights[i] // pool), surplus)
            holding[i] = holding[i] + more
            surplus = surplus - more
    return np.array(holding)


def bell_draw(rng, extent, spread, reach, cuts=(), kind=jnp.bfloat16):
    gain = levels(rng, extent, cuts, -0.22, 0.18) if cuts else 1.0
    array = jax.random.normal(rng, extent, jnp.float32) * spread * gain
    return jnp.minimum(jnp.maximum(array, -reach), reach).astype(kind)


def setup_inputs(seed: int = 0) -> dict:
    key_list = jax.random.split(jax.random.key(seed), 9)
    context = bell_draw(key_list[0], (ROWS, HV), 1.0, 6.0, ((0, 8), (1, 16)))
    attn_weight = bell_draw(key_list[1], (HV, D), HV ** -0.5, 0.0625, ((0, 16), (1, 8)))
    stream = bell_draw(key_list[2], (ROWS, D), 1.0, 6.0, ((0, 128),))
    norm_gain = jnp.clip(1.0 + 0.18 * jax.random.normal(key_list[3], (D,), jnp.float32), 0.1, 1.9)
    router_weight = bell_draw(key_list[4], (EXPERTS, D), D ** -0.5, 0.078125)
    expert_weights = bell_draw(key_list[5], (EXPERTS, 3, FF, D), D ** -0.5, 0.078125, ((0, 16), (2, 8)))
    inference_slot = jax.random.permutation(key_list[6], EXPERTS).astype(jnp.int32)
    routes_keys = jax.random.split(jax.random.fold_in(key_list[7], 1), ROWS // ROWS_DEV)
    routes_turns = jax.random.permutation(jax.random.fold_in(key_list[7], 3), ROWS // ROWS_DEV)
    routes = jax.vmap(lambda own, number: shared_out(jax.random.fold_in(key_list[7], 2), own, number, ROWS_DEV, EXPERTS, TOP, CAP, 2))(routes_keys, routes_turns).reshape((ROWS, TOP))
    return {"context": context, "attn_weight": attn_weight, "stream": stream, "norm_gain": norm_gain, "router_weight": router_weight, "expert_weights": expert_weights, "inference_slot": inference_slot, "routes": routes}


def reference(context, attn_weight, stream, norm_gain, router_weight, expert_weights, inference_slot, routes):
    attended = jnp.dot(context, attn_weight, preferred_element_type=jnp.float32)
    hidden = (stream.astype(jnp.float32) + attended).astype(jnp.bfloat16)
    widened = hidden.astype(jnp.float32)
    normed = (widened * lax.rsqrt(lax.optimization_barrier(jnp.mean(widened * widened, axis=1, keepdims=True)) + 1e-06) * norm_gain).astype(jnp.bfloat16)
    scores = jax.nn.sigmoid(jnp.dot(normed, router_weight.T, preferred_element_type=jnp.float32))
    chosen = jnp.take_along_axis(scores, routes, axis=1)
    share = 2.5 * chosen / lax.optimization_barrier(jnp.sum(chosen, axis=1, keepdims=True))
    expert_ids = jnp.arange(EXPERTS, dtype=jnp.int32)
    source = lax.optimization_barrier(jnp.sum(jnp.where(inference_slot[:, None] == expert_ids[None, :], expert_ids[:, None], 0), axis=0)).astype(jnp.int32)
    placed = jnp.take(expert_weights, source, axis=0)
    flat_ids = routes.reshape(-1)
    slot_count = N_DP * N_MP * CAP
    row_index = (jnp.arange(flat_ids.shape[0], dtype=jnp.int32) // TOP).astype(jnp.int32)
    group_width = FF // N_DP

    def one_expert(running, expert):
        is_mine = flat_ids == expert
        position = (jnp.cumsum(is_mine.astype(jnp.int32)) - 1).astype(jnp.int32)
        target = jnp.where(is_mine, position, slot_count).astype(jnp.int32)
        picked = jnp.zeros((slot_count,), jnp.int32).at[target].set(row_index, mode='drop')
        row_data = normed[picked].astype(jnp.float32)
        expert_set = lax.dynamic_index_in_dim(placed, expert, 0, keepdims=False).astype(jnp.float32)
        gate_part = jnp.dot(row_data, expert_set[0].T, precision=lax.Precision.HIGHEST)
        up_part = jnp.dot(row_data, expert_set[1].T, precision=lax.Precision.HIGHEST)
        active = lax.optimization_barrier((jax.nn.silu(gate_part) * up_part).astype(jnp.bfloat16)).astype(jnp.float32)
        groups = active.reshape(slot_count, N_DP, group_width)
        down_part = expert_set[2].reshape(N_DP, group_width, D)
        partial_value = jnp.einsum('rjf,jfd->rjd', groups, down_part, precision=lax.Precision.HIGHEST)
        partial_value = lax.optimization_barrier(partial_value.astype(jnp.bfloat16)).astype(jnp.float32)
        answer = lax.optimization_barrier(jnp.sum(partial_value, axis=1)).astype(jnp.bfloat16)
        fetched = answer[jnp.clip(position, 0, slot_count - 1)].astype(jnp.float32)
        return (running + jnp.where(is_mine[:, None], fetched, jnp.float32(0.0)), None)
    start = jnp.zeros((flat_ids.shape[0], D), jnp.float32)
    gathered, unused = lax.scan(one_expert, start, expert_ids)
    per_choice = gathered.reshape(ROWS, TOP, D)
    expert_mix = lax.optimization_barrier(jnp.sum(share[:, :, None] * per_choice, axis=1)).astype(jnp.bfloat16)
    return (hidden, expert_mix, placed)
```

```python
import functools

import jax
import jax.numpy as jnp
from jax import lax
from jax.experimental import pallas as pl
from jax.experimental.pallas import tpu as pltpu
from jax.sharding import PartitionSpec as P

Z_LO, CHIPS_X, CORES = 2, 4, 2
SHIFTS = ((0, 1), (0, 3), (1, 0), (0, 2), (1, 1), (1, 3), (1, 2))


def chip_pairs(dz, dx):
    pairs = []
    for i in range(Z_LO * CHIPS_X * CORES):
        z, x, core = i // (CHIPS_X * CORES), (i // CORES) % CHIPS_X, i % CORES
        to = (((z + dz) % Z_LO) * CHIPS_X + (x + dx) % CHIPS_X) * CORES + core
        pairs.append((i, to))
    return pairs


CORE_PAIRS = [(i, i ^ 1) for i in range(Z_LO * CHIPS_X * CORES)]


def placing_kernel(sources, meta, chooser, own, *refs):
    blocks, swapped, out = refs[: sources - 1], refs[sources - 1], refs[sources]
    held, ready, in_sem, out_sem = refs[sources + 1 :]
    parts, rows, slots, width = ready.shape
    me = meta[0]
    core = lax.rem(me, CORES)
    chip = me // CORES
    lead = pl.multiple_of(8 * core, 8)
    copies = []
    for k in range(sources):
        if k == 0:
            ref = own.at[:, pl.ds(pl.multiple_of(chip * 2 * rows + lead, 8), 16), :]
        else:
            ref = blocks[k - 1].at[:, pl.ds(lead, 16), :]
        copies.append(pltpu.make_async_copy(ref, held.at[:, k], in_sem.at[k]))
        copies.append(
            pltpu.make_async_copy(
                swapped.at[k], held.at[:, sources + k], in_sem.at[sources + k]
            )
        )
    for copy in copies:
        copy.start()
    for copy in copies:
        copy.wait()
    outward = [
        pltpu.make_async_copy(ready.at[part], out.at[part], out_sem.at[part])
        for part in range(parts)
    ]
    chunk = 512
    for part in range(parts):

        def step(at, carry, part=part):
            columns = pl.ds(pl.multiple_of(at * chunk, chunk), chunk)
            block = held[part, :, :, columns].reshape(2 * sources * 16, chunk)
            picked = jnp.dot(chooser[...], block, preferred_element_type=jnp.float32)
            ready[part, :, :, columns] = picked.astype(ready.dtype).reshape(rows, slots, chunk)
            return carry

        lax.fori_loop(0, width // chunk, step, 0)
        outward[part].start()
    for copy in outward:
        copy.wait()


def placed_blocks(me, inference_slot, own, blocks, swapped):
    sources = len(blocks) + 1
    parts, units, width = own.shape
    slots = 2 * sources
    rows = units // slots
    core, chip = me % CORES, me // CORES
    z, x = chip // CHIPS_X, chip % CHIPS_X
    came = []
    for core_from in (core, 1 - core):
        for dz, dx in ((0, 0),) + SHIFTS:
            chip_from = ((z + Z_LO - dz) % Z_LO) * CHIPS_X + (x + CHIPS_X - dx) % CHIPS_X
            came.append(chip_from * CORES + core_from)
    came = jnp.stack(came)
    ids = jnp.arange(slots, dtype=jnp.int32)
    goes = jnp.sum(jnp.where(came[:, None] == ids[None, :], inference_slot[None, :], 0), axis=1)
    chooser = (
        (jnp.arange(rows)[:, None, None, None] + 4 * core == jnp.arange(16)[None, None, None, :])
        & (ids[None, :, None, None] == goes[None, None, :, None])
    ).astype(own.dtype).reshape(rows * slots, slots * 16)
    any_space = pl.BlockSpec(memory_space=pl.ANY)
    placed = pl.pallas_call(
        functools.partial(placing_kernel, sources),
        out_shape=jax.ShapeDtypeStruct((parts, rows, slots, width), own.dtype),
        in_specs=[
            pl.BlockSpec(memory_space=pltpu.SMEM),
            pl.BlockSpec(memory_space=pltpu.VMEM),
        ]
        + [any_space] * (sources + 1),
        out_specs=any_space,
        scratch_shapes=[
            pltpu.VMEM((parts, slots, 16, width), own.dtype),
            pltpu.VMEM((parts, rows, slots, width), own.dtype),
            pltpu.SemaphoreType.DMA((slots,)),
            pltpu.SemaphoreType.DMA((parts,)),
        ],
        compiler_params=pltpu.CompilerParams(vmem_limit_bytes=24 << 20),
        cost_estimate=pl.CostEstimate(flops=2 << 30, bytes_accessed=16 << 20, transcendentals=0),
        name="placing",
    )(me[None].astype(jnp.int32), chooser, own, *blocks, swapped)
    return jnp.transpose(placed, (2, 0, 1, 3))


def chip_slice(own, chip, rows):
    return lax.dynamic_slice_in_dim(own, chip * rows, rows, axis=1)


def moved_experts(own, inference_slot):
    me = lax.axis_index("mp")
    core, chip = me % CORES, me // CORES
    z, x = chip // CHIPS_X, chip % CHIPS_X
    chips = Z_LO * CHIPS_X
    rows = own.shape[1] // chips
    sent = []
    for dz, dx in SHIFTS:
        to = ((z + dz) % Z_LO) * CHIPS_X + (x + dx) % CHIPS_X
        sent.append(chip_slice(own, to, rows))
    sent = lax.optimization_barrier(sent)
    blocks = []
    for n, (shift, block) in enumerate(zip(SHIFTS, sent)):
        with jax.named_scope(f"xmove{n}"):
            blocks.append(lax.ppermute(block, "mp", chip_pairs(*shift)))
    other = 8 * (1 - core)
    shared = [lax.dynamic_slice_in_dim(own, chip * rows + other, 16, axis=1)]
    shared += [lax.dynamic_slice_in_dim(block, other, 16, axis=1) for block in blocks]
    with jax.named_scope("xswap"):
        swapped = lax.ppermute(jnp.stack(shared), "mp", CORE_PAIRS)
    return placed_blocks(me, inference_slot, own, blocks, swapped)


def expert_apply(row_block, expert_set):
    contract = (((1,), (1,)), ((), ()))
    gate_part = lax.dot_general(
        row_block, expert_set[0], contract, preferred_element_type=jnp.float32
    )
    up_part = lax.dot_general(
        row_block, expert_set[1], contract, preferred_element_type=jnp.float32
    )
    active = (jax.nn.silu(gate_part) * up_part).astype(jnp.bfloat16)
    return jnp.dot(active, expert_set[2], preferred_element_type=jnp.float32)


def per_device(
    context, attn_weight, stream, norm_gain, router_weight, expert_weights, inference_slot, routes
):
    mp_count = lax.axis_size("mp")
    dp_count = lax.axis_size("dp")
    row_count = stream.shape[0]
    model_width = stream.shape[1]
    top_count = routes.shape[1]
    capacity = 2
    expert_ids = jnp.arange(mp_count, dtype=jnp.int32)
    source = jnp.sum(
        jnp.where(inference_slot[:, None] == expert_ids[None, :], expert_ids[:, None], 0), axis=0
    )
    placed = moved_experts(expert_weights[0], inference_slot)
    column_width = attn_weight.shape[1]
    with jax.named_scope("ctx"):
        gathered = lax.all_to_all(
            jnp.broadcast_to(context[None], (dp_count, *context.shape)), "dp", 0, 0, tiled=True
        )
    partial_value = jnp.dot(
        gathered.reshape(-1, context.shape[1]), attn_weight, preferred_element_type=jnp.float32
    ).astype(jnp.bfloat16)
    partial_value = partial_value.reshape(dp_count * mp_count, row_count, column_width)
    with jax.named_scope("heads"):
        summed = lax.all_to_all(partial_value, ("dp", "mp"), 0, 0, tiled=True)
    summed = summed.reshape(dp_count, mp_count, row_count, column_width)
    attended = jnp.sum(summed, axis=1, dtype=jnp.float32)
    attended = jnp.moveaxis(attended, 0, 1).reshape(row_count, model_width)
    hidden = (stream.astype(jnp.float32) + attended).astype(jnp.bfloat16)
    widened = hidden.astype(jnp.float32)
    normed = (
        widened * lax.rsqrt(jnp.mean(widened * widened, axis=1, keepdims=True) + 1e-06) * norm_gain
    ).astype(jnp.bfloat16)
    logits = lax.dot_general(
        normed, router_weight, (((1,), (1,)), ((), ())), preferred_element_type=jnp.float32
    )
    scores = jax.nn.sigmoid(logits)
    matches = routes[:, :, None] == expert_ids[None, None, :]
    chosen = jnp.sum(jnp.where(matches, scores[:, None, :], 0.0), axis=2)
    share = 2.5 * chosen / jnp.sum(chosen, axis=1, keepdims=True)
    destination = jnp.sum(jnp.where(matches, source[None, None, :], 0), axis=2).reshape(-1)
    onehot = (destination[:, None] == expert_ids[None, :]).astype(jnp.int32)
    earlier = jnp.cumsum(onehot, axis=0) - onehot
    position = jnp.sum(earlier * onehot, axis=1)
    slot_index = destination * capacity + position
    slot_ids = jnp.arange(mp_count * capacity, dtype=jnp.int32)
    placing = (slot_index[:, None] == slot_ids[None, :]).astype(jnp.float32)
    row_ids = jnp.arange(row_count * top_count, dtype=jnp.int32) // top_count
    row_owner = (row_ids[:, None] == jnp.arange(row_count, dtype=jnp.int32)[None, :]).astype(
        jnp.float32
    )
    pick_matrix = jnp.dot(placing.T, row_owner, precision=lax.Precision.HIGHEST).astype(
        jnp.bfloat16
    )
    outgoing = jnp.dot(pick_matrix, normed, preferred_element_type=jnp.float32).astype(jnp.bfloat16)
    outgoing = outgoing.reshape(mp_count, capacity, model_width)
    combine_matrix = jnp.dot(
        row_owner.T, placing * share.reshape(-1)[:, None], precision=lax.Precision.HIGHEST
    )
    local_expert = expert_weights[0]
    copies = jnp.broadcast_to(outgoing[None], (dp_count,) + outgoing.shape).reshape(
        dp_count * mp_count, capacity, model_width
    )
    with jax.named_scope("dispatch"):
        arrived = lax.all_to_all(copies, ("dp", "mp"), split_axis=0, concat_axis=0, tiled=True)
    partial_out = (
        expert_apply(arrived.reshape(-1, model_width), local_expert)
        .astype(jnp.bfloat16)
        .reshape(arrived.shape)
    )
    with jax.named_scope("giveback"):
        returned = lax.all_to_all(partial_out, ("dp", "mp"), split_axis=0, concat_axis=0, tiled=True)
    returned = returned.reshape(dp_count, mp_count, capacity, model_width)
    results = jnp.sum(returned, axis=0, dtype=jnp.float32).astype(jnp.bfloat16)
    expert_mix = jnp.dot(
        combine_matrix,
        results.reshape(-1, model_width).astype(jnp.float32),
        precision=lax.Precision.HIGHEST,
    ).astype(jnp.bfloat16)
    return (hidden, expert_mix, placed)


def solution(mesh):
    placed = (
        P("dp", "mp"),
        P("mp", "dp"),
        P(("dp", "mp"), None),
        P(),
        P(),
        P("mp", None, "dp", None),
        P(),
        P(("dp", "mp"), None),
    )
    return jax.shard_map(
        per_device,
        mesh=mesh,
        in_specs=placed,
        out_specs=(P(("dp", "mp"), None), P(("dp", "mp"), None), P(None, None, ("dp", "mp"), None)),
        check_vma=False,
    )
```

```python
import functools

import jax
import jax.numpy as jnp
from jax import lax
from jax.experimental import pallas as pl
from jax.experimental.pallas import tpu as pltpu
from jax.sharding import PartitionSpec as P


Z_LO, CHIPS_X, CORES = 2, 4, 2
CHIPS_Y, Z_HI = 4, 2
EARLY = 3
SHIFTS = ((0, 1), (0, 3), (1, 0), (0, 2), (1, 1), (1, 3), (1, 2))


def chip_pairs(dz, dx):
    pairs = []
    for i in range(Z_LO * CHIPS_X * CORES):
        z, x, core = i // (CHIPS_X * CORES), (i // CORES) % CHIPS_X, i % CORES
        to = (((z + dz) % Z_LO) * CHIPS_X + (x + dx) % CHIPS_X) * CORES + core
        pairs.append((i, to))
    return pairs


CORE_PAIRS = [(i, i ^ 1) for i in range(Z_LO * CHIPS_X * CORES)]


def placing_kernel(count, meta, chooser, *refs):
    blocks, out = refs[:count], refs[count]
    held, ready, in_sem, out_sem = refs[count + 1 :]
    parts, rows, slots, width = ready.shape
    lead = pl.multiple_of(8 * lax.rem(meta[0], CORES), 8)
    copies = []
    for part in range(parts):
        for k in range(count):
            ref = blocks[k].at[part, pl.ds(lead, 16), :]
            copies.append(pltpu.make_async_copy(ref, held.at[part, k], in_sem.at[part, k]))
    for copy in copies:
        copy.start()
    outward = [
        pltpu.make_async_copy(ready.at[part], out.at[part], out_sem.at[part])
        for part in range(parts)
    ]
    chunk = 1024
    for part in range(parts):
        for copy in copies[part * count : (part + 1) * count]:
            copy.wait()

        def step(at, carry, part=part):
            columns = pl.ds(pl.multiple_of(at * chunk, chunk), chunk)
            block = held[part, :, :, columns].reshape(count * 16, chunk)
            picked = jnp.dot(chooser[...], block, preferred_element_type=jnp.float32)
            ready[part, :, :, columns] = picked.astype(ready.dtype).reshape(rows, slots, chunk)
            return carry

        lax.fori_loop(0, width // chunk, step, 0)
        outward[part].start()
    for copy in outward:
        copy.wait()


def placed_blocks(me, inference_slot, blocks):
    slots = len(blocks)
    parts, rows, width = blocks[0].shape
    rows = rows // CORES
    core, chip = me % CORES, me // CORES
    z, x = chip // CHIPS_X, chip % CHIPS_X
    came = []
    for core_from in (core, 1 - core):
        for dz, dx in ((0, 0),) + SHIFTS:
            chip_from = ((z + Z_LO - dz) % Z_LO) * CHIPS_X + (x + CHIPS_X - dx) % CHIPS_X
            came.append(chip_from * CORES + core_from)
    came = jnp.stack(came)
    ids = jnp.arange(slots, dtype=jnp.int32)
    goes = jnp.sum(jnp.where(came[:, None] == ids[None, :], inference_slot[None, :], 0), axis=1)
    chooser = (
        (jnp.arange(rows)[:, None, None, None] + 4 * core == jnp.arange(16)[None, None, None, :])
        & (ids[None, :, None, None] == goes[None, None, :, None])
    ).astype(blocks[0].dtype).reshape(rows * slots, slots * 16)
    any_space = pl.BlockSpec(memory_space=pl.ANY)
    placed = pl.pallas_call(
        functools.partial(placing_kernel, slots),
        out_shape=jax.ShapeDtypeStruct((parts, rows, slots, width), blocks[0].dtype),
        in_specs=[
            pl.BlockSpec(memory_space=pltpu.SMEM),
            pl.BlockSpec(memory_space=pltpu.VMEM),
        ]
        + [any_space] * slots,
        out_specs=pl.BlockSpec(memory_space=pltpu.HBM),
        scratch_shapes=[
            pltpu.VMEM((parts, slots, 16, width), blocks[0].dtype),
            pltpu.VMEM((parts, rows, slots, width), blocks[0].dtype),
            pltpu.SemaphoreType.DMA((parts, slots)),
            pltpu.SemaphoreType.DMA((parts,)),
        ],
        compiler_params=pltpu.CompilerParams(vmem_limit_bytes=16 << 20),
        cost_estimate=pl.CostEstimate(flops=2 << 30, bytes_accessed=16 << 20, transcendentals=0),
        name="placing",
    )(me[None].astype(jnp.int32), chooser, *blocks)
    return jnp.transpose(placed, (2, 0, 1, 3))


def copy_kernel(source, out):
    out[...] = source[...]


def passed_on(array):
    shape = array.shape
    array = array.reshape(-1, shape[-1])
    return pl.pallas_call(
        copy_kernel,
        out_shape=jax.ShapeDtypeStruct(array.shape, array.dtype),
        in_specs=[pl.BlockSpec(memory_space=pltpu.VMEM)],
        out_specs=pl.BlockSpec(memory_space=pltpu.VMEM),
    )(array).reshape(shape)


def chip_slice(own, chip, rows):
    return lax.dynamic_slice_in_dim(own, chip * rows, rows, axis=1)


def moved_experts(own, inference_slot):
    me = lax.axis_index("mp")
    chip = me // CORES
    z, x = chip // CHIPS_X, chip % CHIPS_X
    chips = Z_LO * CHIPS_X
    rows = own.shape[1] // chips
    sent = []
    for dz, dx in SHIFTS:
        to = ((z + dz) % Z_LO) * CHIPS_X + (x + dx) % CHIPS_X
        sent.append(chip_slice(own, to, rows))
    sent = lax.optimization_barrier(sent[:EARLY]) + lax.optimization_barrier(sent[EARLY:])
    blocks = []
    for shift, block in zip(SHIFTS, sent):
        blocks.append(lax.ppermute(block, "mp", chip_pairs(*shift)))
    mine = chip_slice(own, chip, rows)
    swapped = []
    for block in [mine] + blocks:
        swapped.append(lax.ppermute(block, "mp", CORE_PAIRS))
    me = passed_on(me[None].astype(jnp.int32))[0]
    return placed_blocks(me, inference_slot, [mine] + blocks + swapped)


def expert_kernel(count, *refs):
    blocks, weights, outs = refs[:count], refs[count], refs[count + 1 : 2 * count + 1]
    rows_in, held, ready, row_sem, weight_sem, out_sem = refs[2 * count + 1 :]
    block_rows = blocks[0].shape[0]
    width = rows_in.shape[1]
    arrive = [
        pltpu.make_async_copy(
            blocks[n], rows_in.at[pl.ds(n * block_rows, block_rows), :], row_sem.at[n]
        )
        for n in range(count)
    ]
    fetch = [
        pltpu.make_async_copy(weights.at[part], held.at[part], weight_sem.at[part])
        for part in range(3)
    ]
    for copy in arrive + fetch:
        copy.start()
    for copy in arrive:
        copy.wait()
    contract = (((1,), (1,)), ((), ()))
    sums = []
    for part in range(2):
        fetch[part].wait()
        sums.append(
            lax.dot_general(
                rows_in[...], held[part], contract, preferred_element_type=jnp.float32
            )
        )
    opened, scale = sums
    active = (opened / (1.0 + jnp.exp(-opened)) * scale).astype(jnp.bfloat16)
    fetch[2].wait()
    chunk = 1024
    outward = []
    for at in range(width // chunk):
        columns = pl.ds(at * chunk, chunk)
        ready[:, columns] = jnp.dot(
            active, held[2, :, columns], preferred_element_type=jnp.float32
        ).astype(jnp.bfloat16)
        for n in range(count):
            copy = pltpu.make_async_copy(
                ready.at[pl.ds(n * block_rows, block_rows), columns],
                outs[n].at[:, columns],
                out_sem.at[at, n],
            )
            copy.start()
            outward.append(copy)
    for copy in outward:
        copy.wait()


def expert_apply(blocks, weights):
    count = len(blocks)
    block_rows, width = blocks[0].shape
    total = count * block_rows
    any_space = pl.BlockSpec(memory_space=pl.ANY)
    in_hbm = pl.BlockSpec(memory_space=pltpu.HBM)
    return pl.pallas_call(
        functools.partial(expert_kernel, count),
        out_shape=[jax.ShapeDtypeStruct((block_rows, width), jnp.bfloat16)] * count,
        in_specs=[any_space] * count + [in_hbm],
        out_specs=[in_hbm] * count,
        scratch_shapes=[
            pltpu.VMEM((total, width), jnp.bfloat16),
            pltpu.VMEM(weights.shape, jnp.bfloat16),
            pltpu.VMEM((total, width), jnp.bfloat16),
            pltpu.SemaphoreType.DMA((count,)),
            pltpu.SemaphoreType.DMA((3,)),
            pltpu.SemaphoreType.DMA((width // 1024, count)),
        ],
        compiler_params=pltpu.CompilerParams(vmem_limit_bytes=16 << 20),
        cost_estimate=pl.CostEstimate(flops=4 << 30, bytes_accessed=12 << 20, transcendentals=0),
        name="experts",
    )(*blocks, weights)


def row_pairs(dy, dz):
    return [(d, (d // Z_HI + dy) % CHIPS_Y * Z_HI + (d + dz) % Z_HI) for d in range(CHIPS_Y * Z_HI)]


TURNS_Y = (1, 3, 2)


def rows_of_all(own):
    other = lax.ppermute(own, "dp", row_pairs(0, 1))
    groups = []
    for block in (own, other):
        groups.append([block])
        for dy in TURNS_Y:
            groups[-1].append(lax.ppermute(block, "dp", row_pairs(dy, 0)))
    return groups[0] + groups[1]


def added(blocks):
    total = blocks[0].astype(jnp.float32)
    for block in blocks[1:]:
        total = total + block.astype(jnp.float32)
    return total.astype(jnp.bfloat16)


def sums_at_owner(partials):
    half = len(partials) // 2
    sums = []
    for turn in (1, 0):
        blocks = partials[turn * half : (turn + 1) * half]
        came = [blocks[0]]
        for dy, block in zip(TURNS_Y, blocks[1:]):
            came.append(lax.ppermute(block, "dp", row_pairs(-dy, 0)))
        if turn:
            sums.append(lax.ppermute(added(came), "dp", row_pairs(0, 1)))
        else:
            sums += came
    return added(sums)


def handoff(
    context, attn_weight, stream, norm_gain, router_weight, expert_weights, inference_slot, routes
):
    mp_count = lax.axis_size("mp")
    dp_count = lax.axis_size("dp")
    row_count = stream.shape[0]
    model_width = stream.shape[1]
    top_count = routes.shape[1]
    capacity = 2
    expert_ids = jnp.arange(mp_count, dtype=jnp.int32)
    source = jnp.sum(
        jnp.where(inference_slot[:, None] == expert_ids[None, :], expert_ids[:, None], 0), axis=0
    )
    inference_slot = passed_on(inference_slot[None])[0]
    routes = passed_on(routes)
    placed = moved_experts(expert_weights[0], inference_slot)
    column_width = attn_weight.shape[1]
    gathered = lax.all_to_all(
        jnp.broadcast_to(context[None], (dp_count, *context.shape)), "dp", 0, 0, tiled=True
    )
    partial_value = jnp.dot(
        gathered.reshape(-1, context.shape[1]), attn_weight, preferred_element_type=jnp.float32
    ).astype(jnp.bfloat16)
    partial_value = partial_value.reshape(dp_count * mp_count, row_count, column_width)
    summed = lax.all_to_all(partial_value, ("dp", "mp"), 0, 0, tiled=True)
    summed = summed.reshape(dp_count, mp_count, row_count, column_width)
    attended = jnp.sum(summed, axis=1, dtype=jnp.float32)
    attended = jnp.moveaxis(attended, 0, 1).reshape(row_count, model_width)
    hidden = (stream.astype(jnp.float32) + attended).astype(jnp.bfloat16)
    widened = hidden.astype(jnp.float32)
    normed = (
        widened * lax.rsqrt(jnp.mean(widened * widened, axis=1, keepdims=True) + 1e-06) * norm_gain
    ).astype(jnp.bfloat16)
    logits = lax.dot_general(
        normed, router_weight, (((1,), (1,)), ((), ())), preferred_element_type=jnp.float32
    )
    scores = jax.nn.sigmoid(logits)
    matches = routes[:, :, None] == expert_ids[None, None, :]
    chosen = jnp.sum(jnp.where(matches, scores[:, None, :], 0.0), axis=2)
    share = 2.5 * chosen / jnp.sum(chosen, axis=1, keepdims=True)
    destination = jnp.sum(jnp.where(matches, source[None, None, :], 0), axis=2).reshape(-1)
    onehot = (destination[:, None] == expert_ids[None, :]).astype(jnp.int32)
    earlier = jnp.cumsum(onehot, axis=0) - onehot
    position = jnp.sum(earlier * onehot, axis=1)
    slot_index = destination * capacity + position
    slot_ids = jnp.arange(mp_count * capacity, dtype=jnp.int32)
    placing = (slot_index[:, None] == slot_ids[None, :]).astype(jnp.float32)
    row_ids = jnp.arange(row_count * top_count, dtype=jnp.int32) // top_count
    row_owner = (row_ids[:, None] == jnp.arange(row_count, dtype=jnp.int32)[None, :]).astype(
        jnp.float32
    )
    pick_matrix = jnp.dot(placing.T, row_owner, precision=lax.Precision.HIGHEST).astype(
        jnp.bfloat16
    )
    outgoing = jnp.dot(pick_matrix, normed, preferred_element_type=jnp.float32).astype(jnp.bfloat16)
    outgoing = outgoing.reshape(mp_count, capacity, model_width)
    combine_matrix = jnp.dot(
        row_owner.T, placing * share.reshape(-1)[:, None], precision=lax.Precision.HIGHEST
    )
    own_rows = lax.all_to_all(outgoing, "mp", split_axis=0, concat_axis=0, tiled=True)
    blocks = rows_of_all(own_rows.reshape(-1, model_width))
    partials = expert_apply(blocks, expert_weights[0])
    answer = sums_at_owner(partials).reshape(mp_count, capacity, model_width)
    returned = lax.all_to_all(answer, "mp", split_axis=0, concat_axis=0, tiled=True)
    expert_mix = jnp.dot(
        combine_matrix,
        returned.reshape(-1, model_width).astype(jnp.float32),
        precision=lax.Precision.HIGHEST,
    ).astype(jnp.bfloat16)
    return (hidden, expert_mix, placed)


def solution(mesh):
    placed = (
        P("dp", "mp"),
        P("mp", "dp"),
        P(("dp", "mp"), None),
        P(),
        P(),
        P("mp", None, "dp", None),
        P(),
        P(("dp", "mp"), None),
    )
    return jax.shard_map(
        handoff,
        mesh=mesh,
        in_specs=placed,
        out_specs=(P(("dp", "mp"), None), P(("dp", "mp"), None), P(None, None, ("dp", "mp"), None)),
        check_vma=False,
    )
```

```python
import functools

import jax
import jax.numpy as jnp
from jax import lax
from jax.experimental import pallas as pl
from jax.experimental.pallas import tpu as pltpu
from jax.sharding import PartitionSpec as P


Z_LO, CHIPS_X, CORES = 2, 4, 2
CHIPS_Y, Z_HI = 4, 2
EARLY = 3
SHIFTS = ((0, 1), (0, 3), (1, 0), (0, 2), (1, 1), (1, 3), (1, 2))


def chip_pairs(dz, dx):
    pairs = []
    for i in range(Z_LO * CHIPS_X * CORES):
        z, x, core = i // (CHIPS_X * CORES), (i // CORES) % CHIPS_X, i % CORES
        to = (((z + dz) % Z_LO) * CHIPS_X + (x + dx) % CHIPS_X) * CORES + core
        pairs.append((i, to))
    return pairs


CORE_PAIRS = [(i, i ^ 1) for i in range(Z_LO * CHIPS_X * CORES)]


def placing_kernel(count, meta, chooser, *refs):
    blocks, out = refs[:count], refs[count]
    held, ready, in_sem, out_sem = refs[count + 1 :]
    parts, rows, slots, width = ready.shape
    lead = pl.multiple_of(8 * lax.rem(meta[0], CORES), 8)
    copies = []
    for part in range(parts):
        for k in range(count):
            ref = blocks[k].at[part, pl.ds(lead, 16), :]
            copies.append(pltpu.make_async_copy(ref, held.at[part, k], in_sem.at[part, k]))
    for copy in copies:
        copy.start()
    outward = [
        pltpu.make_async_copy(ready.at[part], out.at[part], out_sem.at[part])
        for part in range(parts)
    ]
    chunk = 1024
    for part in range(parts):
        for copy in copies[part * count : (part + 1) * count]:
            copy.wait()

        def step(at, carry, part=part):
            columns = pl.ds(pl.multiple_of(at * chunk, chunk), chunk)
            block = held[part, :, :, columns].reshape(count * 16, chunk)
            picked = jnp.dot(chooser[...], block, preferred_element_type=jnp.float32)
            ready[part, :, :, columns] = picked.astype(ready.dtype).reshape(rows, slots, chunk)
            return carry

        lax.fori_loop(0, width // chunk, step, 0, unroll=True)
        outward[part].start()
    for copy in outward:
        copy.wait()


def placed_blocks(me, inference_slot, blocks):
    slots = len(blocks)
    parts, rows, width = blocks[0].shape
    rows = rows // CORES
    core, chip = me % CORES, me // CORES
    z, x = chip // CHIPS_X, chip % CHIPS_X
    came = []
    for core_from in (core, 1 - core):
        for dz, dx in ((0, 0),) + SHIFTS:
            chip_from = ((z + Z_LO - dz) % Z_LO) * CHIPS_X + (x + CHIPS_X - dx) % CHIPS_X
            came.append(chip_from * CORES + core_from)
    came = jnp.stack(came)
    ids = jnp.arange(slots, dtype=jnp.int32)
    goes = jnp.sum(jnp.where(came[:, None] == ids[None, :], inference_slot[None, :], 0), axis=1)
    chooser = (
        (jnp.arange(rows)[:, None, None, None] + 4 * core == jnp.arange(16)[None, None, None, :])
        & (ids[None, :, None, None] == goes[None, None, :, None])
    ).astype(blocks[0].dtype).reshape(rows * slots, slots * 16)
    any_space = pl.BlockSpec(memory_space=pl.ANY)
    placed = pl.pallas_call(
        functools.partial(placing_kernel, slots),
        out_shape=jax.ShapeDtypeStruct((parts, rows, slots, width), blocks[0].dtype),
        in_specs=[
            pl.BlockSpec(memory_space=pltpu.SMEM),
            pl.BlockSpec(memory_space=pltpu.VMEM),
        ]
        + [any_space] * slots,
        out_specs=pl.BlockSpec(memory_space=pltpu.HBM),
        scratch_shapes=[
            pltpu.VMEM((parts, slots, 16, width), blocks[0].dtype),
            pltpu.VMEM((parts, rows, slots, width), blocks[0].dtype),
            pltpu.SemaphoreType.DMA((parts, slots)),
            pltpu.SemaphoreType.DMA((parts,)),
        ],
        compiler_params=pltpu.CompilerParams(vmem_limit_bytes=16 << 20),
        cost_estimate=pl.CostEstimate(flops=2 << 30, bytes_accessed=16 << 20, transcendentals=0),
        name="placing",
    )(me[None].astype(jnp.int32), chooser, *blocks)
    return jnp.transpose(placed, (2, 0, 1, 3))


def copy_kernel(source, out):
    out[...] = source[...]


def passed_on(array):
    shape = array.shape
    array = array.reshape(-1, shape[-1])
    return pl.pallas_call(
        copy_kernel,
        out_shape=jax.ShapeDtypeStruct(array.shape, array.dtype),
        in_specs=[pl.BlockSpec(memory_space=pltpu.VMEM)],
        out_specs=pl.BlockSpec(memory_space=pltpu.VMEM),
    )(array).reshape(shape)


def chip_slice(own, chip, rows):
    return lax.dynamic_slice_in_dim(own, chip * rows, rows, axis=1)


def moved_experts(own, later, inference_slot):
    me = lax.axis_index("mp")
    chip = me // CORES
    z, x = chip // CHIPS_X, chip % CHIPS_X
    chips = Z_LO * CHIPS_X
    rows = own.shape[1] // chips
    sent = []
    for n, (dz, dx) in enumerate(SHIFTS):
        to = ((z + dz) % Z_LO) * CHIPS_X + (x + dx) % CHIPS_X
        sent.append(chip_slice(own if n < EARLY else later, to, rows))
    mine = chip_slice(later, chip, rows)
    sent = lax.optimization_barrier(sent[:EARLY]) + lax.optimization_barrier(sent[EARLY:])
    blocks = []
    for shift, block in zip(SHIFTS, sent):
        blocks.append(lax.ppermute(block, "mp", chip_pairs(*shift)))
    swapped = []
    for block in [mine] + blocks:
        swapped.append(lax.ppermute(block, "mp", CORE_PAIRS))
    me = passed_on(me[None].astype(jnp.int32))
    me = passed_on(me)[0]
    return placed_blocks(me, inference_slot, [mine] + blocks + swapped)


def expert_kernel(count, *refs):
    blocks, weights, outs = refs[:count], refs[count], refs[count + 1 : 2 * count + 1]
    rows_in, held, ready, row_sem, weight_sem, out_sem = refs[2 * count + 1 :]
    block_rows = blocks[0].shape[0]
    width = rows_in.shape[1]
    arrive = [
        pltpu.make_async_copy(
            blocks[n], rows_in.at[pl.ds(n * block_rows, block_rows), :], row_sem.at[n]
        )
        for n in range(count)
    ]
    fetch = [
        pltpu.make_async_copy(weights.at[part], held.at[part], weight_sem.at[part])
        for part in range(3)
    ]
    for copy in arrive + fetch:
        copy.start()
    for copy in arrive:
        copy.wait()
    contract = (((1,), (1,)), ((), ()))
    sums = []
    for part in range(2):
        fetch[part].wait()
        sums.append(
            lax.dot_general(
                rows_in[...], held[part], contract, preferred_element_type=jnp.float32
            )
        )
    opened, scale = sums
    active = (opened / (1.0 + jnp.exp(-opened)) * scale).astype(jnp.bfloat16)
    fetch[2].wait()
    chunk = 1024
    outward = []
    for at in range(width // chunk):
        columns = pl.ds(at * chunk, chunk)
        ready[:, columns] = jnp.dot(
            active, held[2, :, columns], preferred_element_type=jnp.float32
        ).astype(jnp.bfloat16)
        for n in range(count):
            copy = pltpu.make_async_copy(
                ready.at[pl.ds(n * block_rows, block_rows), columns],
                outs[n].at[:, columns],
                out_sem.at[at, n],
            )
            copy.start()
            outward.append(copy)
    for copy in outward:
        copy.wait()


def expert_apply(blocks, weights):
    count = len(blocks)
    block_rows, width = blocks[0].shape
    total = count * block_rows
    any_space = pl.BlockSpec(memory_space=pl.ANY)
    in_hbm = pl.BlockSpec(memory_space=pltpu.HBM)
    return pl.pallas_call(
        functools.partial(expert_kernel, count),
        out_shape=[jax.ShapeDtypeStruct((block_rows, width), jnp.bfloat16)] * count,
        in_specs=[any_space] * count + [in_hbm],
        out_specs=[in_hbm] * count,
        scratch_shapes=[
            pltpu.VMEM((total, width), jnp.bfloat16),
            pltpu.VMEM(weights.shape, jnp.bfloat16),
            pltpu.VMEM((total, width), jnp.bfloat16),
            pltpu.SemaphoreType.DMA((count,)),
            pltpu.SemaphoreType.DMA((3,)),
            pltpu.SemaphoreType.DMA((width // 1024, count)),
        ],
        compiler_params=pltpu.CompilerParams(vmem_limit_bytes=58 << 20),
        cost_estimate=pl.CostEstimate(flops=4 << 30, bytes_accessed=12 << 20, transcendentals=0),
        name="experts",
    )(*blocks, weights)


def row_pairs(dy, dz):
    return [(d, (d // Z_HI + dy) % CHIPS_Y * Z_HI + (d + dz) % Z_HI) for d in range(CHIPS_Y * Z_HI)]


TURNS_Y = (1, 3, 2)


def rows_of_all(own):
    other = lax.ppermute(own, "dp", row_pairs(0, 1))
    groups = []
    for block in (own, other):
        groups.append([block])
        for dy in TURNS_Y:
            groups[-1].append(lax.ppermute(block, "dp", row_pairs(dy, 0)))
    return groups


def added(blocks):
    total = blocks[0].astype(jnp.float32)
    for block in blocks[1:]:
        total = total + block.astype(jnp.float32)
    return total.astype(jnp.bfloat16)


def sums_along_y(partials):
    came = [partials[0]]
    for dy, block in zip(TURNS_Y, partials[1:]):
        came.append(lax.ppermute(block, "dp", row_pairs(-dy, 0)))
    return added(came)


def handoff(
    context, attn_weight, stream, norm_gain, router_weight, expert_weights, inference_slot, routes
):
    mp_count = lax.axis_size("mp")
    dp_count = lax.axis_size("dp")
    row_count = stream.shape[0]
    model_width = stream.shape[1]
    top_count = routes.shape[1]
    capacity = 2
    expert_ids = jnp.arange(mp_count, dtype=jnp.int32)
    source = jnp.sum(
        jnp.where(inference_slot[:, None] == expert_ids[None, :], expert_ids[:, None], 0), axis=0
    )
    inference_slot = passed_on(inference_slot[None])[0]
    routes = passed_on(routes)
    column_width = attn_weight.shape[1]
    gathered = lax.all_to_all(
        jnp.broadcast_to(context[None], (dp_count, *context.shape)), "dp", 0, 0, tiled=True
    )
    gathered, later = lax.optimization_barrier((gathered, expert_weights[0]))
    placed = moved_experts(expert_weights[0], later, inference_slot)
    partial_value = jnp.dot(
        gathered.reshape(-1, context.shape[1]), attn_weight, preferred_element_type=jnp.float32
    ).astype(jnp.bfloat16)
    partial_value = partial_value.reshape(dp_count * mp_count, row_count, column_width)
    summed = lax.all_to_all(partial_value, ("dp", "mp"), 0, 0, tiled=True)
    summed = summed.reshape(dp_count, mp_count, row_count, column_width)
    attended = jnp.sum(summed, axis=1, dtype=jnp.float32)
    attended = jnp.moveaxis(attended, 0, 1).reshape(row_count, model_width)
    hidden = (stream.astype(jnp.float32) + attended).astype(jnp.bfloat16)
    widened = hidden.astype(jnp.float32)
    normed = (
        widened * lax.rsqrt(jnp.mean(widened * widened, axis=1, keepdims=True) + 1e-06) * norm_gain
    ).astype(jnp.bfloat16)
    logits = lax.dot_general(
        normed, router_weight, (((1,), (1,)), ((), ())), preferred_element_type=jnp.float32
    )
    scores = jax.nn.sigmoid(logits)
    matches = routes[:, :, None] == expert_ids[None, None, :]
    chosen = jnp.sum(jnp.where(matches, scores[:, None, :], 0.0), axis=2)
    share = 2.5 * chosen / jnp.sum(chosen, axis=1, keepdims=True)
    destination = jnp.sum(jnp.where(matches, source[None, None, :], 0), axis=2).reshape(-1)
    onehot = (destination[:, None] == expert_ids[None, :]).astype(jnp.int32)
    earlier = jnp.cumsum(onehot, axis=0) - onehot
    position = jnp.sum(earlier * onehot, axis=1)
    slot_index = destination * capacity + position
    slot_ids = jnp.arange(mp_count * capacity, dtype=jnp.int32)
    placing = (slot_index[:, None] == slot_ids[None, :]).astype(jnp.float32)
    row_ids = jnp.arange(row_count * top_count, dtype=jnp.int32) // top_count
    row_owner = (row_ids[:, None] == jnp.arange(row_count, dtype=jnp.int32)[None, :]).astype(
        jnp.float32
    )
    pick_matrix = jnp.dot(placing.T, row_owner, precision=lax.Precision.HIGHEST).astype(
        jnp.bfloat16
    )
    outgoing = jnp.dot(pick_matrix, normed, preferred_element_type=jnp.float32).astype(jnp.bfloat16)
    outgoing = outgoing.reshape(mp_count, capacity, model_width)
    combine_matrix = jnp.dot(
        row_owner.T, placing * share.reshape(-1)[:, None], precision=lax.Precision.HIGHEST
    )
    own_rows = lax.all_to_all(outgoing, "mp", split_axis=0, concat_axis=0, tiled=True)
    groups = rows_of_all(own_rows.reshape(-1, model_width))
    sums = []
    for blocks in groups:
        partials = expert_apply(blocks, expert_weights[0])
        sums.append(sums_along_y(partials))
    first = lax.axis_index("dp") % Z_HI == 0
    answer = jnp.stack([jnp.where(first, sums[0], sums[1]), jnp.where(first, sums[1], sums[0])])
    answer = answer.reshape(Z_HI * mp_count, capacity, model_width)
    teams = [
        [(y * Z_HI + z) * mp_count + m for z in range(Z_HI) for m in range(mp_count)]
        for y in range(CHIPS_Y)
    ]
    returned = lax.all_to_all(
        answer, ("dp", "mp"), 0, 0, axis_index_groups=teams, tiled=True
    )
    expert_mix = jnp.dot(
        jnp.concatenate([combine_matrix] * Z_HI, axis=1),
        returned.reshape(-1, model_width).astype(jnp.float32),
        precision=lax.Precision.HIGHEST,
    ).astype(jnp.bfloat16)
    return (hidden, expert_mix, placed)


def solution(mesh):
    placed = (
        P("dp", "mp"),
        P("mp", "dp"),
        P(("dp", "mp"), None),
        P(),
        P(),
        P("mp", None, "dp", None),
        P(),
        P(("dp", "mp"), None),
    )
    return jax.shard_map(
        handoff,
        mesh=mesh,
        in_specs=placed,
        out_specs=(P(("dp", "mp"), None), P(("dp", "mp"), None), P(None, None, ("dp", "mp"), None)),
        check_vma=False,
    )
```

```python
import functools

import jax
import jax.numpy as jnp
from jax import lax
from jax.experimental import pallas as pl
from jax.experimental.pallas import tpu as pltpu
from jax.sharding import PartitionSpec as P


Z_LO, CHIPS_X, CORES = 2, 4, 2
CHIPS_Y, Z_HI = 4, 2
EARLY = 3
SHIFTS = ((0, 1), (0, 3), (1, 0), (0, 2), (1, 1), (1, 3), (1, 2))


def chip_pairs(dz, dx):
    pairs = []
    for i in range(Z_LO * CHIPS_X * CORES):
        z, x, core = i // (CHIPS_X * CORES), (i // CORES) % CHIPS_X, i % CORES
        to = (((z + dz) % Z_LO) * CHIPS_X + (x + dx) % CHIPS_X) * CORES + core
        pairs.append((i, to))
    return pairs


CORE_PAIRS = [(i, i ^ 1) for i in range(Z_LO * CHIPS_X * CORES)]


def placing_kernel(count, meta, goes, *refs):
    blocks, out = refs[:count], refs[count]
    held, ready, in_sem, out_sem = refs[count + 1 :]
    parts, rows, slots, width = ready.shape
    lead = pl.multiple_of(8 * lax.rem(meta[0], CORES), 8)
    copies = []
    for part in range(parts):
        for k in range(count):
            ref = blocks[k].at[part, pl.ds(lead, 16), :]
            copies.append(pltpu.make_async_copy(ref, held.at[part, k], in_sem.at[part, k]))
    for copy in copies:
        copy.start()
    column = lax.broadcasted_iota(jnp.int32, (rows * slots, count * 16), 1)
    line = lax.broadcasted_iota(jnp.int32, (rows * slots, count * 16), 0)
    target = jnp.zeros_like(column)
    for k in range(count):
        target = jnp.where(column // 16 == k, goes[k], target)
    chooser = (
        (line // slots + 4 * lax.rem(meta[0], CORES) == column % 16) & (line % slots == target)
    ).astype(ready.dtype)
    outward = [
        pltpu.make_async_copy(ready.at[part], out.at[part], out_sem.at[part])
        for part in range(parts)
    ]
    chunk = 1024
    for part in range(parts):
        for copy in copies[part * count : (part + 1) * count]:
            copy.wait()

        def step(at, carry, part=part):
            columns = pl.ds(pl.multiple_of(at * chunk, chunk), chunk)
            block = held[part, :, :, columns].reshape(count * 16, chunk)
            picked = jnp.dot(chooser, block, preferred_element_type=jnp.float32)
            ready[part, :, :, columns] = picked.astype(ready.dtype).reshape(rows, slots, chunk)
            return carry

        lax.fori_loop(0, width // chunk, step, 0, unroll=True)
        outward[part].start()
    for copy in outward:
        copy.wait()


def placed_blocks(me, inference_slot, blocks):
    slots = len(blocks)
    parts, rows, width = blocks[0].shape
    rows = rows // CORES
    core, chip = me % CORES, me // CORES
    z, x = chip // CHIPS_X, chip % CHIPS_X
    came = []
    for core_from in (core, 1 - core):
        for dz, dx in ((0, 0),) + SHIFTS:
            chip_from = ((z + Z_LO - dz) % Z_LO) * CHIPS_X + (x + CHIPS_X - dx) % CHIPS_X
            came.append(chip_from * CORES + core_from)
    came = jnp.stack(came)
    ids = jnp.arange(slots, dtype=jnp.int32)
    goes = jnp.sum(jnp.where(came[:, None] == ids[None, :], inference_slot[None, :], 0), axis=1)
    any_space = pl.BlockSpec(memory_space=pl.ANY)
    placed = pl.pallas_call(
        functools.partial(placing_kernel, slots),
        out_shape=jax.ShapeDtypeStruct((parts, rows, slots, width), blocks[0].dtype),
        in_specs=[
            pl.BlockSpec(memory_space=pltpu.SMEM),
            pl.BlockSpec(memory_space=pltpu.SMEM),
        ]
        + [any_space] * slots,
        out_specs=pl.BlockSpec(memory_space=pltpu.HBM),
        scratch_shapes=[
            pltpu.VMEM((parts, slots, 16, width), blocks[0].dtype),
            pltpu.VMEM((parts, rows, slots, width), blocks[0].dtype),
            pltpu.SemaphoreType.DMA((parts, slots)),
            pltpu.SemaphoreType.DMA((parts,)),
        ],
        compiler_params=pltpu.CompilerParams(vmem_limit_bytes=16 << 20),
        cost_estimate=pl.CostEstimate(flops=2 << 30, bytes_accessed=16 << 20, transcendentals=0),
        name="placing",
    )(me[None].astype(jnp.int32), goes, *blocks)
    return jnp.transpose(placed, (2, 0, 1, 3))


def copy_kernel(source, out):
    out[...] = source[...]


def passed_on(array):
    shape = array.shape
    array = array.reshape(-1, shape[-1])
    return pl.pallas_call(
        copy_kernel,
        out_shape=jax.ShapeDtypeStruct(array.shape, array.dtype),
        in_specs=[pl.BlockSpec(memory_space=pltpu.VMEM)],
        out_specs=pl.BlockSpec(memory_space=pltpu.VMEM),
    )(array).reshape(shape)


def chip_slice(own, chip, rows):
    return lax.dynamic_slice_in_dim(own, chip * rows, rows, axis=1)


def moved_experts(own, later, inference_slot):
    me = lax.axis_index("mp")
    chip = me // CORES
    z, x = chip // CHIPS_X, chip % CHIPS_X
    chips = Z_LO * CHIPS_X
    rows = own.shape[1] // chips
    sent = []
    for n, (dz, dx) in enumerate(SHIFTS):
        to = ((z + dz) % Z_LO) * CHIPS_X + (x + dx) % CHIPS_X
        sent.append(chip_slice(own if n < EARLY else later, to, rows))
    mine = chip_slice(later, chip, rows)
    sent = lax.optimization_barrier(sent[:EARLY]) + lax.optimization_barrier(sent[EARLY:])
    blocks = []
    for shift, block in zip(SHIFTS, sent):
        blocks.append(lax.ppermute(block, "mp", chip_pairs(*shift)))
    swapped = []
    for block in [mine] + blocks:
        swapped.append(lax.ppermute(block, "mp", CORE_PAIRS))
    me = passed_on(me[None].astype(jnp.int32))
    me = passed_on(me)[0]
    return placed_blocks(me, inference_slot, [mine] + blocks + swapped)


def expert_kernel(count, *refs):
    blocks, weights, outs = refs[:count], refs[count], refs[count + 1 : 2 * count + 1]
    rows_in, held, ready, row_sem, weight_sem, out_sem = refs[2 * count + 1 :]
    block_rows = blocks[0].shape[0]
    width = rows_in.shape[1]
    arrive = [
        pltpu.make_async_copy(
            blocks[n], rows_in.at[pl.ds(n * block_rows, block_rows), :], row_sem.at[n]
        )
        for n in range(count)
    ]
    fetch = [
        pltpu.make_async_copy(weights.at[part], held.at[part], weight_sem.at[part])
        for part in range(3)
    ]
    for copy in arrive + fetch:
        copy.start()
    for copy in arrive:
        copy.wait()
    contract = (((1,), (1,)), ((), ()))
    sums = []
    for part in range(2):
        fetch[part].wait()
        sums.append(
            lax.dot_general(
                rows_in[...], held[part], contract, preferred_element_type=jnp.float32
            )
        )
    opened, scale = sums
    active = (opened / (1.0 + jnp.exp(-opened)) * scale).astype(jnp.bfloat16)
    fetch[2].wait()
    chunk = 1024
    outward = []
    for at in range(width // chunk):
        columns = pl.ds(at * chunk, chunk)
        ready[:, columns] = jnp.dot(
            active, held[2, :, columns], preferred_element_type=jnp.float32
        ).astype(jnp.bfloat16)
        for n in range(count):
            copy = pltpu.make_async_copy(
                ready.at[pl.ds(n * block_rows, block_rows), columns],
                outs[n].at[:, columns],
                out_sem.at[at, n],
            )
            copy.start()
            outward.append(copy)
    for copy in outward:
        copy.wait()


def expert_apply(blocks, weights):
    count = len(blocks)
    block_rows, width = blocks[0].shape
    total = count * block_rows
    any_space = pl.BlockSpec(memory_space=pl.ANY)
    in_hbm = pl.BlockSpec(memory_space=pltpu.HBM)
    return pl.pallas_call(
        functools.partial(expert_kernel, count),
        out_shape=[jax.ShapeDtypeStruct((block_rows, width), jnp.bfloat16)] * count,
        in_specs=[any_space] * count + [in_hbm],
        out_specs=[in_hbm] * count,
        scratch_shapes=[
            pltpu.VMEM((total, width), jnp.bfloat16),
            pltpu.VMEM(weights.shape, jnp.bfloat16),
            pltpu.VMEM((total, width), jnp.bfloat16),
            pltpu.SemaphoreType.DMA((count,)),
            pltpu.SemaphoreType.DMA((3,)),
            pltpu.SemaphoreType.DMA((width // 1024, count)),
        ],
        compiler_params=pltpu.CompilerParams(vmem_limit_bytes=58 << 20),
        cost_estimate=pl.CostEstimate(flops=4 << 30, bytes_accessed=12 << 20, transcendentals=0),
        name="experts",
    )(*blocks, weights)


def row_pairs(dy, dz):
    return [(d, (d // Z_HI + dy) % CHIPS_Y * Z_HI + (d + dz) % Z_HI) for d in range(CHIPS_Y * Z_HI)]


TURNS_Y = (1, 3, 2)


def rows_of_all(own):
    other = lax.ppermute(own, "dp", row_pairs(0, 1))
    groups = []
    for block in (own, other):
        groups.append([block])
        for dy in TURNS_Y:
            groups[-1].append(lax.ppermute(block, "dp", row_pairs(dy, 0)))
    return groups


def added(blocks):
    total = blocks[0].astype(jnp.float32)
    for block in blocks[1:]:
        total = total + block.astype(jnp.float32)
    return total.astype(jnp.bfloat16)


def sums_along_y(partials):
    came = [partials[0]]
    for dy, block in zip(TURNS_Y, partials[1:]):
        came.append(lax.ppermute(block, "dp", row_pairs(-dy, 0)))
    return added(came)


def handoff(
    context, attn_weight, stream, norm_gain, router_weight, expert_weights, inference_slot, routes
):
    mp_count = lax.axis_size("mp")
    dp_count = lax.axis_size("dp")
    row_count = stream.shape[0]
    model_width = stream.shape[1]
    top_count = routes.shape[1]
    capacity = 2
    expert_ids = jnp.arange(mp_count, dtype=jnp.int32)
    source = jnp.sum(
        jnp.where(inference_slot[:, None] == expert_ids[None, :], expert_ids[:, None], 0), axis=0
    )
    inference_slot = passed_on(inference_slot[None])[0]
    routes = passed_on(routes)
    column_width = attn_weight.shape[1]
    gathered = lax.all_to_all(
        jnp.broadcast_to(context[None], (dp_count, *context.shape)), "dp", 0, 0, tiled=True
    )
    gathered, later = lax.optimization_barrier((gathered, expert_weights[0]))
    placed = moved_experts(expert_weights[0], later, inference_slot)
    partial_value = jnp.dot(
        gathered.reshape(-1, context.shape[1]), attn_weight, preferred_element_type=jnp.float32
    ).astype(jnp.bfloat16)
    partial_value = partial_value.reshape(dp_count * mp_count, row_count, column_width)
    summed = lax.all_to_all(partial_value, ("dp", "mp"), 0, 0, tiled=True)
    summed = summed.reshape(dp_count, mp_count, row_count, column_width)
    attended = jnp.sum(summed, axis=1, dtype=jnp.float32)
    attended = jnp.moveaxis(attended, 0, 1).reshape(row_count, model_width)
    hidden = (stream.astype(jnp.float32) + attended).astype(jnp.bfloat16)
    widened = hidden.astype(jnp.float32)
    normed = (
        widened * lax.rsqrt(jnp.mean(widened * widened, axis=1, keepdims=True) + 1e-06) * norm_gain
    ).astype(jnp.bfloat16)
    logits = lax.dot_general(
        normed, router_weight, (((1,), (1,)), ((), ())), preferred_element_type=jnp.float32
    )
    scores = jax.nn.sigmoid(logits)
    matches = routes[:, :, None] == expert_ids[None, None, :]
    chosen = jnp.sum(jnp.where(matches, scores[:, None, :], 0.0), axis=2)
    share = 2.5 * chosen / jnp.sum(chosen, axis=1, keepdims=True)
    destination = jnp.sum(jnp.where(matches, source[None, None, :], 0), axis=2).reshape(-1)
    onehot = (destination[:, None] == expert_ids[None, :]).astype(jnp.int32)
    earlier = jnp.cumsum(onehot, axis=0) - onehot
    position = jnp.sum(earlier * onehot, axis=1)
    slot_index = destination * capacity + position
    slot_ids = jnp.arange(mp_count * capacity, dtype=jnp.int32)
    placing = (slot_index[:, None] == slot_ids[None, :]).astype(jnp.float32)
    row_ids = jnp.arange(row_count * top_count, dtype=jnp.int32) // top_count
    row_owner = (row_ids[:, None] == jnp.arange(row_count, dtype=jnp.int32)[None, :]).astype(
        jnp.float32
    )
    pick_matrix = jnp.dot(placing.T, row_owner, precision=lax.Precision.HIGHEST).astype(
        jnp.bfloat16
    )
    outgoing = jnp.dot(pick_matrix, normed, preferred_element_type=jnp.float32).astype(jnp.bfloat16)
    outgoing = outgoing.reshape(mp_count, capacity, model_width)
    combine_matrix = jnp.dot(
        row_owner.T, placing * share.reshape(-1)[:, None], precision=lax.Precision.HIGHEST
    )
    combine_matrix = passed_on(jnp.concatenate([combine_matrix] * Z_HI, axis=1))
    own_rows = lax.all_to_all(outgoing, "mp", split_axis=0, concat_axis=0, tiled=True)
    groups = rows_of_all(own_rows.reshape(-1, model_width))
    sums = []
    for turn, blocks in enumerate(groups):
        partials = expert_apply(blocks, expert_weights[0])
        sums.append(lax.optimization_barrier(sums_along_y(partials)) if turn == 0 else sums_along_y(partials))
    first = lax.axis_index("dp") % Z_HI == 0
    answer = jnp.stack([jnp.where(first, sums[0], sums[1]), jnp.where(first, sums[1], sums[0])])
    answer = answer.reshape(Z_HI * mp_count, capacity, model_width)
    teams = [
        [(y * Z_HI + z) * mp_count + m for z in range(Z_HI) for m in range(mp_count)]
        for y in range(CHIPS_Y)
    ]
    returned = lax.all_to_all(
        answer, ("dp", "mp"), 0, 0, axis_index_groups=teams, tiled=True
    )
    expert_mix = jnp.dot(
        combine_matrix,
        returned.reshape(-1, model_width).astype(jnp.float32),
        precision=lax.Precision.HIGHEST,
    ).astype(jnp.bfloat16)
    return (hidden, expert_mix, placed)


def solution(mesh):
    placed = (
        P("dp", "mp"),
        P("mp", "dp"),
        P(("dp", "mp"), None),
        P(),
        P(),
        P("mp", None, "dp", None),
        P(),
        P(("dp", "mp"), None),
    )
    return jax.shard_map(
        handoff,
        mesh=mesh,
        in_specs=placed,
        out_specs=(P(("dp", "mp"), None), P(("dp", "mp"), None), P(None, None, ("dp", "mp"), None)),
        check_vma=False,
    )
```
